32 devices in a mesh: row: 4 (over y, x), col: 8 (over z, core).
Axes of the slice: x: 2, y: 2, z: 4, core: 2. Of those that a mesh axis runs over, the one named last changes fastest.
Arguments:
- intensity: float32 [16, 2048, 2048], P(None, 'row', 'col'), may hold values from -6 to 6
- punch_radius: int32 [2, 129, 129], replicated, may hold values from 0 to 12
Outputs:
- out_re: float32 [16, 2048, 2048], P(None, ('row', 'col'))
- out_im: float32 [16, 2048, 2048], P(None, ('row', 'col'))
The draws below stay inside these ranges and needn't reach their ends.
Inputs may be any that keep to these rules, and one draw needn't show every extreme that they name: `punch_radius`: squared radius in voxels; 0 leaves a node unpunched.
All inputs are finite; a program needn't handle non-finite values.
Results may differ from the reference program's by a relative error of at most 0.0029.
Values may be sent and summed in bfloat16 or wider, within the bound.
A program may use at most 128 MiB of HBM per device.

```python
import math
import jax
import jax.numpy as jnp
from jax import lax

N = 2048
SP = 16
L = 16
NODES = 128
LNODES = 2


def plant(array, own_key, smallest, largest):
    longest = array.shape.index(max(array.shape))
    spots = []
    for shift in (0, 1):
        where = [jax.random.randint(jax.random.fold_in(own_key, axis), (), 0, length) for axis, length in enumerate(array.shape)]
        where[longest] = (where[longest] + shift) % array.shape[longest]
        spots.append(tuple(where))
    return array.at[spots[0]].set(smallest).at[spots[1]].set(largest)


def block_scale(key, shape, cuts, least, high):
    gain = 1.0
    for position, parts in cuts:
        heights = jax.random.uniform(jax.random.fold_in(jax.random.fold_in(key, 6), position), (parts,), jnp.float32, least / len(cuts), high / len(cuts))
        gain = gain * jnp.repeat(jnp.exp(heights), shape[position] // parts).reshape((-1,) + (1,) * (len(shape) - 1 - position))
    return gain


def noise(key, extent, scale, reach, pieces=(), held_as=jnp.bfloat16):
    gain = block_scale(key, extent, pieces, -0.22, 0.18) if pieces else 1.0
    array = jax.random.normal(key, extent, jnp.float32) * scale * gain
    return jnp.minimum(jnp.maximum(array, -reach), reach).astype(held_as)


def setup_inputs(seed: int = 0) -> dict:
    splits = jax.random.split(jax.random.key(seed), 3)
    return {
        "intensity": noise(splits[0], (L, N, N), 1.0, 6.0, ((1, 4), (2, 8)), jnp.float32),
        "punch_radius": plant(jax.random.randint(splits[1], (LNODES, NODES + 1, NODES + 1), 0, 13), jax.random.fold_in(splits[1], 1), 0, 12).astype(jnp.int32),
    }


def circle(count, period, width):
    first_ids = jnp.arange(count, dtype=jnp.int32)
    second_ids = jnp.arange(width, dtype=jnp.int32)
    phases = (first_ids[:, None] * second_ids[None, :]) % period
    angles = phases.astype(jnp.float32) * (2.0 * math.pi / period)
    return jnp.cos(angles), jnp.sin(angles)


def mixed(form, left, right):
    return jnp.einsum(form, left, right, precision=lax.Precision.HIGHEST)


def spectral(real_in, imag_in):
    length = real_in.shape[-1]
    first = 32
    second = length // first
    shape_lead = real_in.shape[:-1]
    cos_first, sin_first = circle(first, first, first)
    cos_twist, sin_twist = circle(first, length, second)
    cos_second, sin_second = circle(second, second, second)
    grid_re = real_in.reshape(shape_lead + (first, second))
    section_re = mixed('...ab,ac->...cb', grid_re, cos_first)
    section_im = mixed('...ab,ac->...cb', grid_re, sin_first)
    if imag_in is not None:
        grid_im = imag_in.reshape(shape_lead + (first, second))
        section_re = section_re - mixed('...ab,ac->...cb', grid_im, sin_first)
        section_im = section_im + mixed('...ab,ac->...cb', grid_im, cos_first)
    twist_re = section_re * cos_twist - section_im * sin_twist
    twist_im = section_re * sin_twist + section_im * cos_twist
    final_re = mixed('...cb,bd->...dc', twist_re, cos_second) - mixed('...cb,bd->...dc', twist_im, sin_second)
    final_im = mixed('...cb,bd->...dc', twist_re, sin_second) + mixed('...cb,bd->...dc', twist_im, cos_second)
    return final_re.reshape(shape_lead + (length,)), final_im.reshape(shape_lead + (length,))


def reference(intensity, punch_radius):
    coords = jnp.arange(N, dtype=jnp.int32)
    node_of = (coords + SP // 2) // SP
    offsets = coords - SP * node_of
    dist_sq = offsets[:, None] * offsets[:, None] + offsets[None, :] * offsets[None, :]

    def plane(inputs):
        levels, values = inputs
        plane_node = (levels + SP // 2) // SP
        plane_off = levels - SP * plane_node
        radius_plane = punch_radius[plane_node]
        radius = radius_plane[node_of[:, None], node_of[None, :]]
        keep_mask = (dist_sq + plane_off * plane_off >= radius).astype(jnp.float32)
        keep_swap = keep_mask.T
        counts = jnp.maximum(keep_mask + keep_swap, 1.0)
        symmetric = ((keep_mask * values + keep_swap * values.T) / counts).astype(jnp.bfloat16)
        part_re, part_im = spectral(symmetric.astype(jnp.float32), None)
        real_out, imag_out = spectral(part_re.T, part_im.T)
        return real_out / N, imag_out / N

    plane_ids = jnp.arange(L, dtype=jnp.int32)
    out_re, out_im = lax.map(plane, (plane_ids, intensity))
    return out_re, out_im
```

```python
import math

import jax
import jax.numpy as jnp
from jax import lax
from jax.experimental import pallas as pl
from jax.experimental.pallas import tpu as pltpu
from jax.sharding import PartitionSpec as P

N = 2048
SP = 16


def circle(count, period, width):
    first_ids = jnp.arange(count, dtype=jnp.int32)
    second_ids = jnp.arange(width, dtype=jnp.int32)
    phases = first_ids[:, None] * second_ids[None, :] % period
    angles = phases.astype(jnp.float32) * (2.0 * math.pi / period)
    return (jnp.cos(angles), jnp.sin(angles))


def mixed(form, left, right):
    return jnp.einsum(form, left, right, precision=lax.Precision.HIGHEST)


def spectral(real_in, imag_in):
    length = real_in.shape[-1]
    first = 32
    second = length // first
    shape_lead = real_in.shape[:-1]
    cos_first, sin_first = circle(first, first, first)
    cos_twist, sin_twist = circle(first, length, second)
    cos_second, sin_second = circle(second, second, second)
    grid_re = real_in.reshape(shape_lead + (first, second))
    section_re = mixed("...ab,ac->...cb", grid_re, cos_first)
    section_im = mixed("...ab,ac->...cb", grid_re, sin_first)
    grid_im = imag_in.reshape(shape_lead + (first, second))
    section_re = section_re - mixed("...ab,ac->...cb", grid_im, sin_first)
    section_im = section_im + mixed("...ab,ac->...cb", grid_im, cos_first)
    twist_re = section_re * cos_twist - section_im * sin_twist
    twist_im = section_re * sin_twist + section_im * cos_twist
    final_re = mixed("...cb,bd->...dc", twist_re, cos_second) - mixed(
        "...cb,bd->...dc", twist_im, sin_second
    )
    final_im = mixed("...cb,bd->...dc", twist_re, sin_second) + mixed(
        "...cb,bd->...dc", twist_im, cos_second
    )
    return (final_re.reshape(shape_lead + (length,)), final_im.reshape(shape_lead + (length,)))


def spectral_lead(real_in):
    row_total, length = real_in.shape
    first = 32
    second = length // first
    cos_first, sin_first = circle(first, first, first)
    cos_twist, sin_twist = circle(first, length, second)
    cos_second, sin_second = circle(second, second, second)
    grid_re = real_in.reshape(row_total, first, second)
    section_re = mixed("rab,ac->cbr", grid_re, cos_first)
    section_im = mixed("rab,ac->cbr", grid_re, sin_first)
    twist_re = section_re * cos_twist[:, :, None] - section_im * sin_twist[:, :, None]
    twist_im = section_re * sin_twist[:, :, None] + section_im * cos_twist[:, :, None]
    final_re = mixed("cbr,bd->dcr", twist_re, cos_second) - mixed(
        "cbr,bd->dcr", twist_im, sin_second
    )
    final_im = mixed("cbr,bd->dcr", twist_re, sin_second) + mixed(
        "cbr,bd->dcr", twist_im, cos_second
    )
    return (final_re.reshape(length, row_total), final_im.reshape(length, row_total))


def keep_map(first_coords, second_coords, radius_table, levels):
    node_count = radius_table.shape[1]
    first_node = (first_coords + SP // 2) // SP
    first_dist = first_coords - SP * first_node
    second_node = (second_coords + SP // 2) // SP
    second_dist = second_coords - SP * second_node
    plane_node = (levels + SP // 2) // SP
    plane_dist = levels - SP * plane_node
    node_ids = jnp.arange(node_count, dtype=jnp.int32)
    pick_first = (first_node[:, None] == node_ids[None, :]).astype(jnp.bfloat16)
    pick_second = (second_node[:, None] == node_ids[None, :]).astype(jnp.bfloat16)
    table_half = jnp.einsum(
        "hn,snm->shm",
        pick_first,
        radius_table.astype(jnp.bfloat16),
        preferred_element_type=jnp.float32,
    ).astype(jnp.bfloat16)
    plane_radius = jnp.einsum(
        "shm,km->shk", table_half, pick_second, preferred_element_type=jnp.float32
    )
    level_ids = jnp.arange(radius_table.shape[0], dtype=jnp.int32)
    pick_plane = (plane_node[:, None] == level_ids[None, :]).astype(jnp.float32)
    radius = jnp.einsum("ls,shk->hlk", pick_plane, plane_radius, precision=lax.Precision.HIGHEST)
    distance = (
        (first_dist * first_dist)[:, None, None]
        + (plane_dist * plane_dist)[None, :, None]
        + (second_dist * second_dist)[None, None, :]
    )
    return (distance.astype(jnp.float32) >= radius).astype(jnp.float32)


def pencil_body(intensity, punch_radius):
    row_count = lax.axis_size("row")
    col_count = lax.axis_size("col")
    row_at = lax.axis_index("row")
    col_at = lax.axis_index("col")
    planes, h_block, k_block = intensity.shape
    groups = col_count // row_count
    fine_width = k_block // col_count
    pencil_rows = groups * fine_width
    levels = jnp.arange(planes, dtype=jnp.int32)
    swapped_table = jnp.swapaxes(punch_radius, 1, 2)
    outgoing = jnp.transpose(
        intensity.reshape(planes, h_block, col_count, fine_width), (2, 3, 0, 1)
    )
    arrived = lax.all_to_all(
        lax.all_to_all(outgoing, "col", split_axis=0, concat_axis=0, tiled=True),
        "row",
        split_axis=0,
        concat_axis=3,
        tiled=True,
    )
    pencil_h = (
        h_block * row_at
        + k_block * jnp.arange(groups, dtype=jnp.int32)[:, None]
        + fine_width * col_at
        + jnp.arange(fine_width, dtype=jnp.int32)[None, :]
    ).reshape(-1)
    whole_k = jnp.arange(N, dtype=jnp.int32)
    mirrored = arrived.reshape(pencil_rows, planes, N)
    pencil_input = jnp.transpose(
        intensity.reshape(planes, groups, col_count, fine_width, k_block), (1, 2, 3, 0, 4)
    )
    direct = lax.all_to_all(pencil_input, "col", split_axis=1, concat_axis=4, tiled=True).reshape(
        pencil_rows, planes, N
    )
    keep_mask = keep_map(pencil_h, whole_k, punch_radius, levels)
    keep_swap = keep_map(pencil_h, whole_k, swapped_table, levels)
    counts = jnp.maximum(keep_mask + keep_swap, 1.0)
    symmetric = ((keep_mask * direct + keep_swap * mirrored) / counts).astype(jnp.bfloat16)
    row_total = pencil_rows * planes
    flat_rows = symmetric.reshape(row_total, N).astype(jnp.float32)
    part_re, part_im = spectral_lead(flat_rows)
    freq_width = N // (row_count * col_count)
    sectioned = jnp.stack([part_re, part_im]).reshape(
        2, row_count, col_count, freq_width, row_total
    )
    spectra = lax.all_to_all(
        lax.all_to_all(sectioned, "row", split_axis=1, concat_axis=1, tiled=True),
        "col",
        split_axis=2,
        concat_axis=2,
        tiled=True,
    )
    spectra = spectra.reshape(2, row_count, col_count, freq_width, groups, fine_width, planes)
    spectra = jnp.transpose(spectra, (0, 6, 3, 1, 4, 2, 5)).reshape(2, planes * freq_width, N)
    final_re, final_im = spectral(spectra[0], spectra[1])
    out_re = (final_re / N).reshape(planes, freq_width, N)
    out_im = (final_im / N).reshape(planes, freq_width, N)
    return (out_re, out_im)


RADIX = 4


def spin(first_ids, second_ids, period):
    phases = first_ids * second_ids % period
    angles = phases.astype(jnp.float32) * (2.0 * math.pi / period)
    return jnp.cos(angles), jnp.sin(angles)


def halves(values):
    high = lax.reduce_precision(values, exponent_bits=8, mantissa_bits=7)
    return high.astype(jnp.bfloat16), (values - high).astype(jnp.bfloat16)


def packed(coarse, fine, shape):
    coarse_re, coarse_im = coarse
    fine_re, fine_im = fine
    full_re = (coarse_re * fine_re - coarse_im * fine_im).reshape(shape)
    full_im = (coarse_re * fine_im + coarse_im * fine_re).reshape(shape)
    return jnp.stack([*halves(full_re), *halves(full_im)])


def twiddles(length):
    width = length // RADIX
    fine = 16
    ids = jnp.arange(width, dtype=jnp.int32)
    lead = jnp.arange(RADIX, dtype=jnp.int32)[:, None, None, None]
    high_ids = (jnp.arange(width // fine, dtype=jnp.int32) * fine)[None, :, None, None]
    low_ids = jnp.arange(fine, dtype=jnp.int32)[None, None, :, None]
    minor = ids[None, None, None, :]
    shape = (RADIX, width, width)
    sample = RADIX * minor + lead
    freq_major = packed(spin(sample, high_ids, length), spin(sample, low_ids, length), shape)
    time_major = packed(
        spin(RADIX * high_ids, minor, length), spin(RADIX * low_ids + lead, minor, length), shape
    )
    return freq_major, time_major


def dot32(left, right):
    return jnp.dot(left, right, preferred_element_type=jnp.float32)


def symmetrize(direct_ref, mirror_ref, near_ref, far_ref, pick_ref, order_ref, flip_ref, sym_ref):
    groups, _, block, width = direct_ref.shape
    rows = lax.broadcasted_iota(jnp.int32, (block, width), 0)
    cols = lax.broadcasted_iota(jnp.int32, (block, width), 1)
    row_off = (rows + SP // 2) % SP - SP // 2
    col_off = (cols + SP // 2) % SP - SP // 2
    distance = (row_off * row_off + col_off * col_off).astype(jnp.float32)
    merged = []
    for part in range(groups):
        picked = pick_ref[:, part * width : (part + 1) * width]
        keep_mirror = distance >= dot32(near_ref[0], picked)
        keep_direct = distance >= dot32(far_ref[0], picked)
        turned = jnp.concatenate(
            [
                direct_ref[piece, 0, part * width : (part + 1) * width, :].T
                for piece in range(groups)
            ],
            axis=0,
        )
        total = jnp.where(keep_mirror, mirror_ref[0, part, 0], 0.0) + jnp.where(
            keep_direct, turned, 0.0
        )
        scale = jnp.where(keep_mirror & keep_direct, 0.5, 1.0)
        merged.append((total * scale).astype(jnp.bfloat16))
    sym = jnp.concatenate(merged, axis=1)
    sorted_rows = dot32(order_ref[...], sym).astype(jnp.bfloat16)
    sorted_both = dot32(sorted_rows, flip_ref[...]).astype(jnp.bfloat16)
    sym_ref[0] = sorted_both.reshape(sym_ref.shape[1:])


def butterfly(res, ims):
    even_re, odd_re = res[0] + res[2], res[0] - res[2]
    even_im, odd_im = ims[0] + ims[2], ims[0] - ims[2]
    pair_re, gap_re = res[1] + res[3], res[1] - res[3]
    pair_im, gap_im = ims[1] + ims[3], ims[1] - ims[3]
    out_re = (even_re + pair_re, odd_re - gap_im, even_re - pair_re, odd_re + gap_im)
    out_im = (even_im + pair_im, odd_im + gap_re, even_im - pair_im, odd_im - gap_re)
    return out_re, out_im


def transform_first(table_ref, sym_ref, part_ref):
    res, ims = [], []
    for lead in range(RADIX):
        data = sym_ref[0, lead]
        res.append(dot32(table_ref[0, lead], data) + dot32(table_ref[1, lead], data))
        ims.append(dot32(table_ref[2, lead], data) + dot32(table_ref[3, lead], data))
    out_re, out_im = butterfly(res, ims)
    for block in range(RADIX):
        part_ref[block, 0, 0] = out_re[block].astype(part_ref.dtype)
        part_ref[block, 1, 0] = out_im[block].astype(part_ref.dtype)


def transform_second(scale, part_ref, table_ref, out_ref):
    sources, _, _, _, width = part_ref.shape
    piece = width // RADIX
    res, ims = [], []
    for lead in range(RADIX):
        data_re, data_im = (
            jnp.concatenate(
                [
                    part_ref[source, which, 0, :, lead * piece : (lead + 1) * piece]
                    for source in range(sources)
                ],
                axis=1,
            )
            for which in range(2)
        )
        res.append(
            dot32(data_re, table_ref[0, lead])
            + dot32(data_re, table_ref[1, lead])
            - dot32(data_im, table_ref[2, lead])
            - dot32(data_im, table_ref[3, lead])
        )
        ims.append(
            dot32(data_re, table_ref[2, lead])
            + dot32(data_re, table_ref[3, lead])
            + dot32(data_im, table_ref[0, lead])
            + dot32(data_im, table_ref[1, lead])
        )
    out_re, out_im = butterfly(res, ims)
    owners, _, _, rows, _ = out_ref.shape
    for which, values in ((0, out_re), (1, out_im)):
        for block in range(RADIX):
            ready = (values[block] * scale).astype(out_ref.dtype)
            span = ready.shape[1]
            for owner in range(owners):
                out_ref[owner, which, 0, :, block * span : (block + 1) * span] = ready[
                    owner * rows : (owner + 1) * rows
                ]


LIMIT = 56 * 1024 * 1024


def plane_body(intensity, punch_radius):
    row_count = lax.axis_size("row")
    col_count = lax.axis_size("col")
    row_at = lax.axis_index("row")
    col_at = lax.axis_index("col")
    planes, h_block, k_block = intensity.shape
    held = planes // col_count
    groups = h_block // k_block
    length = h_block * row_count
    width = length // RADIX
    piece = h_block // RADIX
    freq_width = length // (row_count * col_count)
    bf16 = jnp.bfloat16

    direct = lax.all_to_all(intensity, "col", split_axis=0, concat_axis=0, tiled=True)
    mirror = lax.all_to_all(direct, "row", split_axis=0, concat_axis=0, tiled=True)
    direct = direct.reshape(col_count, held, h_block, k_block)
    mirror = mirror.reshape(row_count, groups, held, h_block, k_block)

    levels = held * col_at + jnp.arange(held, dtype=jnp.int32)
    plane_node = (levels + SP // 2) // SP
    plane_off = levels - SP * plane_node
    level_ids = jnp.arange(punch_radius.shape[0], dtype=jnp.int32)
    chosen = (plane_node[:, None] == level_ids[None, :]).astype(jnp.int32)
    table = jnp.sum(chosen[:, :, None, None] * punch_radius[None], axis=1)
    table = (table - (plane_off * plane_off)[:, None, None]).astype(bf16)
    node_count = punch_radius.shape[1]
    node_ids = jnp.arange(node_count, dtype=jnp.int32)
    whole = jnp.arange(length, dtype=jnp.int32)
    pick_k = ((whole[:, None] + SP // 2) // SP == node_ids[None, :]).astype(bf16)
    mine = h_block * row_at + jnp.arange(h_block, dtype=jnp.int32)
    pick_h = ((mine[None, :] + SP // 2) // SP == node_ids[:, None]).astype(bf16)
    near = jnp.einsum("kn,lnm->lkm", pick_k, table, preferred_element_type=jnp.float32)
    far = jnp.einsum("kn,lmn->lkm", pick_k, table, preferred_element_type=jnp.float32)
    near, far = near.astype(bf16), far.astype(bf16)
    local = jnp.arange(h_block, dtype=jnp.int32)
    source = RADIX * (local % piece) + local // piece
    order = (source[:, None] == local[None, :]).astype(bf16)
    flip = (source[None, :] == local[:, None]).astype(bf16)
    freq_major, time_major = twiddles(length)

    sym = pl.pallas_call(
        symmetrize,
        out_shape=jax.ShapeDtypeStruct((held, RADIX, width, h_block), bf16),
        grid=(held, row_count),
        in_specs=[
            pl.BlockSpec((groups, 1, h_block, k_block), lambda p, r: (r, p, 0, 0)),
            pl.BlockSpec((1, groups, 1, h_block, k_block), lambda p, r: (r, 0, p, 0, 0)),
            pl.BlockSpec((1, h_block, node_count), lambda p, r: (p, r, 0)),
            pl.BlockSpec((1, h_block, node_count), lambda p, r: (p, r, 0)),
            pl.BlockSpec((node_count, h_block), lambda p, r: (0, 0)),
            pl.BlockSpec((h_block, h_block), lambda p, r: (0, 0)),
            pl.BlockSpec((h_block, h_block), lambda p, r: (0, 0)),
        ],
        out_specs=pl.BlockSpec((1, RADIX, piece, h_block), lambda p, r: (p, 0, r, 0)),
        compiler_params=pltpu.CompilerParams(vmem_limit_bytes=LIMIT),
    )(direct, mirror, near, far, pick_h, order, flip)

    tile = min(128, width)
    parts = pl.pallas_call(
        transform_first,
        out_shape=jax.ShapeDtypeStruct((RADIX, 2, held, width, h_block), bf16),
        grid=(width // tile, held),
        in_specs=[
            pl.BlockSpec((4, RADIX, tile, width), lambda d, p: (0, 0, d, 0)),
            pl.BlockSpec((1, RADIX, width, h_block), lambda d, p: (p, 0, 0, 0)),
        ],
        out_specs=pl.BlockSpec((RADIX, 2, 1, tile, h_block), lambda d, p: (0, 0, p, d, 0)),
        compiler_params=pltpu.CompilerParams(vmem_limit_bytes=LIMIT),
    )(freq_major, sym)

    parts = lax.all_to_all(parts, "row", split_axis=0, concat_axis=0, tiled=True)

    owners = max(1, tile // freq_width)
    rows = owners * freq_width
    spectra = pl.pallas_call(
        lambda *refs: transform_second(1.0 / length, *refs),
        out_shape=jax.ShapeDtypeStruct((col_count, 2, held, freq_width, length), bf16),
        grid=(held, width // rows),
        in_specs=[
            pl.BlockSpec((row_count, 2, 1, rows, h_block), lambda p, d: (0, 0, p, d, 0)),
            pl.BlockSpec((4, RADIX, width, width), lambda p, d: (0, 0, 0, 0)),
        ],
        out_specs=pl.BlockSpec((owners, 2, 1, freq_width, length), lambda p, d: (d, 0, p, 0, 0)),
        compiler_params=pltpu.CompilerParams(vmem_limit_bytes=LIMIT),
    )(parts, time_major)

    spectra = lax.all_to_all(spectra, "col", split_axis=0, concat_axis=0, tiled=True)
    out_re = spectra[:, 0].reshape(planes, freq_width, length).astype(jnp.float32)
    out_im = spectra[:, 1].reshape(planes, freq_width, length).astype(jnp.float32)
    return out_re, out_im


def body(intensity, punch_radius):
    by_plane = lax.axis_size("row") == RADIX and intensity.shape[0] % lax.axis_size("col") == 0
    return (plane_body if by_plane else pencil_body)(intensity, punch_radius)


def solution(mesh):
    in_specs = (P(None, "row", "col"), P())
    out_specs = (P(None, ("row", "col"), None), P(None, ("row", "col"), None))
    return jax.shard_map(body, mesh=mesh, in_specs=in_specs, out_specs=out_specs, check_vma=False)
```

```python
import math

import jax
import jax.numpy as jnp
from jax import lax
from jax.experimental import pallas as pl
from jax.experimental.pallas import tpu as pltpu
from jax.sharding import PartitionSpec as P

N = 2048
SP = 16


def circle(count, period, width):
    first_ids = jnp.arange(count, dtype=jnp.int32)
    second_ids = jnp.arange(width, dtype=jnp.int32)
    phases = first_ids[:, None] * second_ids[None, :] % period
    angles = phases.astype(jnp.float32) * (2.0 * math.pi / period)
    return (jnp.cos(angles), jnp.sin(angles))


def mixed(form, left, right):
    return jnp.einsum(form, left, right, precision=lax.Precision.HIGHEST)


def spectral(real_in, imag_in):
    length = real_in.shape[-1]
    first = 32
    second = length // first
    shape_lead = real_in.shape[:-1]
    cos_first, sin_first = circle(first, first, first)
    cos_twist, sin_twist = circle(first, length, second)
    cos_second, sin_second = circle(second, second, second)
    grid_re = real_in.reshape(shape_lead + (first, second))
    section_re = mixed("...ab,ac->...cb", grid_re, cos_first)
    section_im = mixed("...ab,ac->...cb", grid_re, sin_first)
    grid_im = imag_in.reshape(shape_lead + (first, second))
    section_re = section_re - mixed("...ab,ac->...cb", grid_im, sin_first)
    section_im = section_im + mixed("...ab,ac->...cb", grid_im, cos_first)
    twist_re = section_re * cos_twist - section_im * sin_twist
    twist_im = section_re * sin_twist + section_im * cos_twist
    final_re = mixed("...cb,bd->...dc", twist_re, cos_second) - mixed(
        "...cb,bd->...dc", twist_im, sin_second
    )
    final_im = mixed("...cb,bd->...dc", twist_re, sin_second) + mixed(
        "...cb,bd->...dc", twist_im, cos_second
    )
    return (final_re.reshape(shape_lead + (length,)), final_im.reshape(shape_lead + (length,)))


def spectral_lead(real_in):
    row_total, length = real_in.shape
    first = 32
    second = length // first
    cos_first, sin_first = circle(first, first, first)
    cos_twist, sin_twist = circle(first, length, second)
    cos_second, sin_second = circle(second, second, second)
    grid_re = real_in.reshape(row_total, first, second)
    section_re = mixed("rab,ac->cbr", grid_re, cos_first)
    section_im = mixed("rab,ac->cbr", grid_re, sin_first)
    twist_re = section_re * cos_twist[:, :, None] - section_im * sin_twist[:, :, None]
    twist_im = section_re * sin_twist[:, :, None] + section_im * cos_twist[:, :, None]
    final_re = mixed("cbr,bd->dcr", twist_re, cos_second) - mixed(
        "cbr,bd->dcr", twist_im, sin_second
    )
    final_im = mixed("cbr,bd->dcr", twist_re, sin_second) + mixed(
        "cbr,bd->dcr", twist_im, cos_second
    )
    return (final_re.reshape(length, row_total), final_im.reshape(length, row_total))


def keep_map(first_coords, second_coords, radius_table, levels):
    node_count = radius_table.shape[1]
    first_node = (first_coords + SP // 2) // SP
    first_dist = first_coords - SP * first_node
    second_node = (second_coords + SP // 2) // SP
    second_dist = second_coords - SP * second_node
    plane_node = (levels + SP // 2) // SP
    plane_dist = levels - SP * plane_node
    node_ids = jnp.arange(node_count, dtype=jnp.int32)
    pick_first = (first_node[:, None] == node_ids[None, :]).astype(jnp.bfloat16)
    pick_second = (second_node[:, None] == node_ids[None, :]).astype(jnp.bfloat16)
    table_half = jnp.einsum(
        "hn,snm->shm",
        pick_first,
        radius_table.astype(jnp.bfloat16),
        preferred_element_type=jnp.float32,
    ).astype(jnp.bfloat16)
    plane_radius = jnp.einsum(
        "shm,km->shk", table_half, pick_second, preferred_element_type=jnp.float32
    )
    level_ids = jnp.arange(radius_table.shape[0], dtype=jnp.int32)
    pick_plane = (plane_node[:, None] == level_ids[None, :]).astype(jnp.float32)
    radius = jnp.einsum("ls,shk->hlk", pick_plane, plane_radius, precision=lax.Precision.HIGHEST)
    distance = (
        (first_dist * first_dist)[:, None, None]
        + (plane_dist * plane_dist)[None, :, None]
        + (second_dist * second_dist)[None, None, :]
    )
    return (distance.astype(jnp.float32) >= radius).astype(jnp.float32)


def pencil_body(intensity, punch_radius):
    row_count = lax.axis_size("row")
    col_count = lax.axis_size("col")
    row_at = lax.axis_index("row")
    col_at = lax.axis_index("col")
    planes, h_block, k_block = intensity.shape
    groups = col_count // row_count
    fine_width = k_block // col_count
    pencil_rows = groups * fine_width
    levels = jnp.arange(planes, dtype=jnp.int32)
    swapped_table = jnp.swapaxes(punch_radius, 1, 2)
    outgoing = jnp.transpose(
        intensity.reshape(planes, h_block, col_count, fine_width), (2, 3, 0, 1)
    )
    arrived = lax.all_to_all(
        lax.all_to_all(outgoing, "col", split_axis=0, concat_axis=0, tiled=True),
        "row",
        split_axis=0,
        concat_axis=3,
        tiled=True,
    )
    pencil_h = (
        h_block * row_at
        + k_block * jnp.arange(groups, dtype=jnp.int32)[:, None]
        + fine_width * col_at
        + jnp.arange(fine_width, dtype=jnp.int32)[None, :]
    ).reshape(-1)
    whole_k = jnp.arange(N, dtype=jnp.int32)
    mirrored = arrived.reshape(pencil_rows, planes, N)
    pencil_input = jnp.transpose(
        intensity.reshape(planes, groups, col_count, fine_width, k_block), (1, 2, 3, 0, 4)
    )
    direct = lax.all_to_all(pencil_input, "col", split_axis=1, concat_axis=4, tiled=True).reshape(
        pencil_rows, planes, N
    )
    keep_mask = keep_map(pencil_h, whole_k, punch_radius, levels)
    keep_swap = keep_map(pencil_h, whole_k, swapped_table, levels)
    counts = jnp.maximum(keep_mask + keep_swap, 1.0)
    symmetric = ((keep_mask * direct + keep_swap * mirrored) / counts).astype(jnp.bfloat16)
    row_total = pencil_rows * planes
    flat_rows = symmetric.reshape(row_total, N).astype(jnp.float32)
    part_re, part_im = spectral_lead(flat_rows)
    freq_width = N // (row_count * col_count)
    sectioned = jnp.stack([part_re, part_im]).reshape(
        2, row_count, col_count, freq_width, row_total
    )
    spectra = lax.all_to_all(
        lax.all_to_all(sectioned, "row", split_axis=1, concat_axis=1, tiled=True),
        "col",
        split_axis=2,
        concat_axis=2,
        tiled=True,
    )
    spectra = spectra.reshape(2, row_count, col_count, freq_width, groups, fine_width, planes)
    spectra = jnp.transpose(spectra, (0, 6, 3, 1, 4, 2, 5)).reshape(2, planes * freq_width, N)
    final_re, final_im = spectral(spectra[0], spectra[1])
    out_re = (final_re / N).reshape(planes, freq_width, N)
    out_im = (final_im / N).reshape(planes, freq_width, N)
    return (out_re, out_im)


RADIX = 4


def spin(first_ids, second_ids, period):
    phases = first_ids * second_ids % period
    angles = phases.astype(jnp.float32) * (2.0 * math.pi / period)
    return jnp.cos(angles), jnp.sin(angles)


def halves(values):
    high = lax.reduce_precision(values, exponent_bits=8, mantissa_bits=7)
    return high.astype(jnp.bfloat16), (values - high).astype(jnp.bfloat16)


def packed(coarse, fine, shape):
    coarse_re, coarse_im = coarse
    fine_re, fine_im = fine
    full_re = (coarse_re * fine_re - coarse_im * fine_im).reshape(shape)
    full_im = (coarse_re * fine_im + coarse_im * fine_re).reshape(shape)
    return jnp.stack([*halves(full_re), *halves(full_im)])


def twiddles(length):
    width = length // RADIX
    fine = 16
    ids = jnp.arange(width, dtype=jnp.int32)
    lead = jnp.arange(RADIX, dtype=jnp.int32)[:, None, None, None]
    high_ids = (jnp.arange(width // fine, dtype=jnp.int32) * fine)[None, :, None, None]
    low_ids = jnp.arange(fine, dtype=jnp.int32)[None, None, :, None]
    minor = ids[None, None, None, :]
    shape = (RADIX, width, width)
    sample = RADIX * minor + lead
    freq_major = packed(spin(sample, high_ids, length), spin(sample, low_ids, length), shape)
    time_major = packed(
        spin(RADIX * high_ids, minor, length), spin(RADIX * low_ids + lead, minor, length), shape
    )
    return freq_major, time_major


def dot32(left, right):
    return jnp.dot(left, right, preferred_element_type=jnp.float32)


def symmetrize(direct_ref, mirror_ref, near_ref, far_ref, pick_ref, order_ref, flip_ref, sym_ref):
    groups, _, block, width = direct_ref.shape
    rows = lax.broadcasted_iota(jnp.int32, (block, width), 0)
    cols = lax.broadcasted_iota(jnp.int32, (block, width), 1)
    row_off = (rows + SP // 2) % SP - SP // 2
    col_off = (cols + SP // 2) % SP - SP // 2
    distance = (row_off * row_off + col_off * col_off).astype(jnp.float32)
    merged = []
    for part in range(groups):
        picked = pick_ref[:, part * width : (part + 1) * width]
        keep_mirror = distance >= dot32(near_ref[0], picked)
        keep_direct = distance >= dot32(far_ref[0], picked)
        turned = jnp.concatenate(
            [
                direct_ref[piece, 0, part * width : (part + 1) * width, :].T
                for piece in range(groups)
            ],
            axis=0,
        )
        total = jnp.where(keep_mirror, mirror_ref[0, part, 0], 0.0) + jnp.where(
            keep_direct, turned, 0.0
        )
        scale = jnp.where(keep_mirror & keep_direct, 0.5, 1.0)
        merged.append((total * scale).astype(jnp.bfloat16))
    sym = jnp.concatenate(merged, axis=1)
    sorted_rows = dot32(order_ref[...], sym).astype(jnp.bfloat16)
    sorted_both = dot32(sorted_rows, flip_ref[...]).astype(jnp.bfloat16)
    sym_ref[0] = sorted_both.reshape(sym_ref.shape[1:])


def butterfly(res, ims):
    even_re, odd_re = res[0] + res[2], res[0] - res[2]
    even_im, odd_im = ims[0] + ims[2], ims[0] - ims[2]
    pair_re, gap_re = res[1] + res[3], res[1] - res[3]
    pair_im, gap_im = ims[1] + ims[3], ims[1] - ims[3]
    out_re = (even_re + pair_re, odd_re - gap_im, even_re - pair_re, odd_re + gap_im)
    out_im = (even_im + pair_im, odd_im + gap_re, even_im - pair_im, odd_im - gap_re)
    return out_re, out_im


def transform_first(table_ref, sym_ref, part_ref):
    res, ims = [], []
    for lead in range(RADIX):
        data = sym_ref[0, lead]
        res.append(dot32(table_ref[0, lead], data) + dot32(table_ref[1, lead], data))
        ims.append(dot32(table_ref[2, lead], data) + dot32(table_ref[3, lead], data))
    out_re, out_im = butterfly(res, ims)
    for block in range(RADIX):
        part_ref[block, 0, 0] = out_re[block].astype(part_ref.dtype)
        part_ref[block, 1, 0] = out_im[block].astype(part_ref.dtype)


def transform_second(scale, part_ref, table_ref, out_ref):
    sources, _, _, _, width = part_ref.shape
    piece = width // RADIX
    res, ims = [], []
    for lead in range(RADIX):
        data_re, data_im = (
            jnp.concatenate(
                [
                    part_ref[source, which, 0, :, lead * piece : (lead + 1) * piece]
                    for source in range(sources)
                ],
                axis=1,
            )
            for which in range(2)
        )
        res.append(
            dot32(data_re, table_ref[0, lead])
            + dot32(data_re, table_ref[1, lead])
            - dot32(data_im, table_ref[2, lead])
            - dot32(data_im, table_ref[3, lead])
        )
        ims.append(
            dot32(data_re, table_ref[2, lead])
            + dot32(data_re, table_ref[3, lead])
            + dot32(data_im, table_ref[0, lead])
            + dot32(data_im, table_ref[1, lead])
        )
    out_re, out_im = butterfly(res, ims)
    owners, _, _, rows, _ = out_ref.shape
    for which, values in ((0, out_re), (1, out_im)):
        for block in range(RADIX):
            ready = (values[block] * scale).astype(out_ref.dtype)
            span = ready.shape[1]
            for owner in range(owners):
                out_ref[owner, which, 0, :, block * span : (block + 1) * span] = ready[
                    owner * rows : (owner + 1) * rows
                ]


def swap_kernel(send_ref, got_ref, stage, send_sem, recv_sem, local_sem):
    count = send_ref.shape[0]
    me = lax.axis_index("row")
    barrier = pltpu.get_barrier_semaphore()
    for step in range(1, count):
        pl.semaphore_signal(barrier, inc=1, device_id={"row": lax.rem(me + step, count)})
    pl.semaphore_wait(barrier, count - 1)
    copies = []
    for step in range(1, count):
        peer = lax.rem(me + step, count)
        copy = pltpu.make_async_remote_copy(
            src_ref=send_ref.at[peer],
            dst_ref=got_ref.at[me],
            send_sem=send_sem.at[step - 1],
            recv_sem=recv_sem.at[step - 1],
            device_id={"row": peer},
        )
        copy.start()
        copies.append(copy)
    load = pltpu.make_async_copy(send_ref.at[me], stage, local_sem.at[0])
    load.start()
    load.wait()
    store = pltpu.make_async_copy(stage, got_ref.at[me], local_sem.at[1])
    store.start()
    store.wait()
    for copy in copies:
        copy.wait()


def swap(values, identity):
    count = values.shape[0]
    return pl.pallas_call(
        swap_kernel,
        out_shape=jax.ShapeDtypeStruct(values.shape, values.dtype),
        in_specs=[pl.BlockSpec(memory_space=pl.ANY)],
        out_specs=pl.BlockSpec(memory_space=pl.ANY),
        scratch_shapes=[
            pltpu.VMEM(values.shape[1:], values.dtype),
            pltpu.SemaphoreType.DMA((count - 1,)),
            pltpu.SemaphoreType.DMA((count - 1,)),
            pltpu.SemaphoreType.DMA((2,)),
        ],
        compiler_params=pltpu.CompilerParams(collective_id=identity, has_side_effects=True),
        cost_estimate=pl.CostEstimate(
            flops=40 * 10**9, bytes_accessed=values.size * 4, transcendentals=0
        ),
    )(values)


def widen_kernel(got_ref, *refs):
    re_ref, im_ref = refs[-2:]
    re_ref[0, 0] = got_ref[0, 0, 0].astype(jnp.float32)
    im_ref[0, 0] = got_ref[0, 1, 0].astype(jnp.float32)


def widen(at, held, received, outs):
    owners, _, _, rows, length = received.shape
    shape = jax.ShapeDtypeStruct((owners, held, rows, length), jnp.float32)
    spec = pl.BlockSpec((1, 1, rows, length), lambda c: (c, at, 0, 0))
    return pl.pallas_call(
        widen_kernel,
        out_shape=(shape, shape),
        grid=(owners,),
        in_specs=[pl.BlockSpec((1, 2, 1, rows, length), lambda c: (c, 0, 0, 0, 0))]
        + [pl.BlockSpec(memory_space=pl.ANY)] * len(outs),
        out_specs=(spec, spec),
        input_output_aliases={1 + which: which for which in range(len(outs))},
        cost_estimate=pl.CostEstimate(
            flops=8 * 10**9, bytes_accessed=received.size * 6, transcendentals=0
        ),
    )(received, *outs)


LIMIT = 56 * 1024 * 1024


def plane_body(intensity, punch_radius):
    row_count = lax.axis_size("row")
    col_count = lax.axis_size("col")
    row_at = lax.axis_index("row")
    col_at = lax.axis_index("col")
    planes, h_block, k_block = intensity.shape
    held = planes // col_count
    groups = h_block // k_block
    length = h_block * row_count
    width = length // RADIX
    piece = h_block // RADIX
    freq_width = length // (row_count * col_count)
    bf16 = jnp.bfloat16

    levels = held * col_at + jnp.arange(held, dtype=jnp.int32)
    plane_node = (levels + SP // 2) // SP
    plane_off = levels - SP * plane_node
    level_ids = jnp.arange(punch_radius.shape[0], dtype=jnp.int32)
    chosen = (plane_node[:, None] == level_ids[None, :]).astype(jnp.int32)
    table = jnp.sum(chosen[:, :, None, None] * punch_radius[None], axis=1)
    table = (table - (plane_off * plane_off)[:, None, None]).astype(bf16)
    node_count = punch_radius.shape[1]
    node_ids = jnp.arange(node_count, dtype=jnp.int32)
    whole = jnp.arange(length, dtype=jnp.int32)
    pick_k = ((whole[:, None] + SP // 2) // SP == node_ids[None, :]).astype(bf16)
    mine = h_block * row_at + jnp.arange(h_block, dtype=jnp.int32)
    pick_h = ((mine[None, :] + SP // 2) // SP == node_ids[:, None]).astype(bf16)
    near = jnp.einsum("kn,lnm->lkm", pick_k, table, preferred_element_type=jnp.float32)
    far = jnp.einsum("kn,lmn->lkm", pick_k, table, preferred_element_type=jnp.float32)
    near, far = near.astype(bf16), far.astype(bf16)
    local = jnp.arange(h_block, dtype=jnp.int32)
    source = RADIX * (local % piece) + local // piece
    order = (source[:, None] == local[None, :]).astype(bf16)
    flip = (source[None, :] == local[:, None]).astype(bf16)
    freq_major, time_major = twiddles(length)

    tile = min(128, width)
    owners = max(1, tile // freq_width)
    rows = owners * freq_width
    params = pltpu.CompilerParams(vmem_limit_bytes=LIMIT)
    split = intensity.reshape(col_count, held, h_block, k_block)

    def gather(at):
        return lax.all_to_all(split[:, at], "col", split_axis=0, concat_axis=0, tiled=True)

    def first(at, direct, mirror):
        sym = pl.pallas_call(
            symmetrize,
            out_shape=jax.ShapeDtypeStruct((1, RADIX, width, h_block), bf16),
            grid=(1, row_count),
            in_specs=[
                pl.BlockSpec((groups, 1, h_block, k_block), lambda p, r: (r, p, 0, 0)),
                pl.BlockSpec((1, groups, 1, h_block, k_block), lambda p, r: (r, 0, p, 0, 0)),
                pl.BlockSpec((1, h_block, node_count), lambda p, r: (p, r, 0)),
                pl.BlockSpec((1, h_block, node_count), lambda p, r: (p, r, 0)),
                pl.BlockSpec((node_count, h_block), lambda p, r: (0, 0)),
                pl.BlockSpec((h_block, h_block), lambda p, r: (0, 0)),
                pl.BlockSpec((h_block, h_block), lambda p, r: (0, 0)),
            ],
            out_specs=pl.BlockSpec((1, RADIX, piece, h_block), lambda p, r: (p, 0, r, 0)),
            compiler_params=params,
            cost_estimate=pl.CostEstimate(
                flops=14 * 10**9, bytes_accessed=10**7, transcendentals=0
            ),
        )(
            direct.reshape(col_count, 1, h_block, k_block),
            mirror.reshape(row_count, groups, 1, h_block, k_block),
            near[at : at + 1],
            far[at : at + 1],
            pick_h,
            order,
            flip,
        )
        return pl.pallas_call(
            transform_first,
            out_shape=jax.ShapeDtypeStruct((RADIX, 2, 1, width, h_block), bf16),
            grid=(width // tile, 1),
            in_specs=[
                pl.BlockSpec((4, RADIX, tile, width), lambda d, p: (0, 0, d, 0)),
                pl.BlockSpec((1, RADIX, width, h_block), lambda d, p: (p, 0, 0, 0)),
            ],
            out_specs=pl.BlockSpec((RADIX, 2, 1, tile, h_block), lambda d, p: (0, 0, p, d, 0)),
            compiler_params=params,
            cost_estimate=pl.CostEstimate(
                flops=14 * 10**9, bytes_accessed=10**7, transcendentals=0
            ),
        )(freq_major, sym)

    def second(parts):
        return pl.pallas_call(
            lambda *refs: transform_second(1.0 / length, *refs),
            out_shape=jax.ShapeDtypeStruct((col_count, 2, 1, freq_width, length), bf16),
            grid=(1, width // rows),
            in_specs=[
                pl.BlockSpec((row_count, 2, 1, rows, h_block), lambda p, d: (0, 0, p, d, 0)),
                pl.BlockSpec((4, RADIX, width, width), lambda p, d: (0, 0, 0, 0)),
            ],
            out_specs=pl.BlockSpec(
                (owners, 2, 1, freq_width, length), lambda p, d: (d, 0, p, 0, 0)
            ),
            compiler_params=params,
            cost_estimate=pl.CostEstimate(
                flops=14 * 10**9, bytes_accessed=10**7, transcendentals=0
            ),
        )(parts, time_major)

    directs = [gather(at) for at in range(held)]
    mirrors = [
        swap(direct.reshape(row_count, groups, h_block, k_block), 0) for direct in directs
    ]
    parts = [swap(first(at, directs[at], mirrors[at]), 1) for at in range(held)]
    spectra = [
        lax.all_to_all(second(part), "col", split_axis=0, concat_axis=0, tiled=True)
        for part in parts
    ]
    outs = ()
    for at, received in enumerate(spectra):
        outs = widen(at, held, received, outs)
    return tuple(half.reshape(planes, freq_width, length) for half in outs)


def body(intensity, punch_radius):
    by_plane = lax.axis_size("row") == RADIX and intensity.shape[0] % lax.axis_size("col") == 0
    return (plane_body if by_plane else pencil_body)(intensity, punch_radius)


def solution(mesh):
    in_specs = (P(None, "row", "col"), P())
    out_specs = (P(None, ("row", "col"), None), P(None, ("row", "col"), None))
    return jax.shard_map(body, mesh=mesh, in_specs=in_specs, out_specs=out_specs, check_vma=False)
```

```python
import math

import jax
import jax.numpy as jnp
from jax import lax
from jax.experimental import pallas as pl
from jax.experimental.pallas import tpu as pltpu
from jax.sharding import PartitionSpec as P

N = 2048
SP = 16


def circle(count, period, width):
    first_ids = jnp.arange(count, dtype=jnp.int32)
    second_ids = jnp.arange(width, dtype=jnp.int32)
    phases = first_ids[:, None] * second_ids[None, :] % period
    angles = phases.astype(jnp.float32) * (2.0 * math.pi / period)
    return (jnp.cos(angles), jnp.sin(angles))


def mixed(form, left, right):
    return jnp.einsum(form, left, right, precision=lax.Precision.HIGHEST)


def spectral(real_in, imag_in):
    length = real_in.shape[-1]
    first = 32
    second = length // first
    shape_lead = real_in.shape[:-1]
    cos_first, sin_first = circle(first, first, first)
    cos_twist, sin_twist = circle(first, length, second)
    cos_second, sin_second = circle(second, second, second)
    grid_re = real_in.reshape(shape_lead + (first, second))
    section_re = mixed("...ab,ac->...cb", grid_re, cos_first)
    section_im = mixed("...ab,ac->...cb", grid_re, sin_first)
    grid_im = imag_in.reshape(shape_lead + (first, second))
    section_re = section_re - mixed("...ab,ac->...cb", grid_im, sin_first)
    section_im = section_im + mixed("...ab,ac->...cb", grid_im, cos_first)
    twist_re = section_re * cos_twist - section_im * sin_twist
    twist_im = section_re * sin_twist + section_im * cos_twist
    final_re = mixed("...cb,bd->...dc", twist_re, cos_second) - mixed(
        "...cb,bd->...dc", twist_im, sin_second
    )
    final_im = mixed("...cb,bd->...dc", twist_re, sin_second) + mixed(
        "...cb,bd->...dc", twist_im, cos_second
    )
    return (final_re.reshape(shape_lead + (length,)), final_im.reshape(shape_lead + (length,)))


def spectral_lead(real_in):
    row_total, length = real_in.shape
    first = 32
    second = length // first
    cos_first, sin_first = circle(first, first, first)
    cos_twist, sin_twist = circle(first, length, second)
    cos_second, sin_second = circle(second, second, second)
    grid_re = real_in.reshape(row_total, first, second)
    section_re = mixed("rab,ac->cbr", grid_re, cos_first)
    section_im = mixed("rab,ac->cbr", grid_re, sin_first)
    twist_re = section_re * cos_twist[:, :, None] - section_im * sin_twist[:, :, None]
    twist_im = section_re * sin_twist[:, :, None] + section_im * cos_twist[:, :, None]
    final_re = mixed("cbr,bd->dcr", twist_re, cos_second) - mixed(
        "cbr,bd->dcr", twist_im, sin_second
    )
    final_im = mixed("cbr,bd->dcr", twist_re, sin_second) + mixed(
        "cbr,bd->dcr", twist_im, cos_second
    )
    return (final_re.reshape(length, row_total), final_im.reshape(length, row_total))


def keep_map(first_coords, second_coords, radius_table, levels):
    node_count = radius_table.shape[1]
    first_node = (first_coords + SP // 2) // SP
    first_dist = first_coords - SP * first_node
    second_node = (second_coords + SP // 2) // SP
    second_dist = second_coords - SP * second_node
    plane_node = (levels + SP // 2) // SP
    plane_dist = levels - SP * plane_node
    node_ids = jnp.arange(node_count, dtype=jnp.int32)
    pick_first = (first_node[:, None] == node_ids[None, :]).astype(jnp.bfloat16)
    pick_second = (second_node[:, None] == node_ids[None, :]).astype(jnp.bfloat16)
    table_half = jnp.einsum(
        "hn,snm->shm",
        pick_first,
        radius_table.astype(jnp.bfloat16),
        preferred_element_type=jnp.float32,
    ).astype(jnp.bfloat16)
    plane_radius = jnp.einsum(
        "shm,km->shk", table_half, pick_second, preferred_element_type=jnp.float32
    )
    level_ids = jnp.arange(radius_table.shape[0], dtype=jnp.int32)
    pick_plane = (plane_node[:, None] == level_ids[None, :]).astype(jnp.float32)
    radius = jnp.einsum("ls,shk->hlk", pick_plane, plane_radius, precision=lax.Precision.HIGHEST)
    distance = (
        (first_dist * first_dist)[:, None, None]
        + (plane_dist * plane_dist)[None, :, None]
        + (second_dist * second_dist)[None, None, :]
    )
    return (distance.astype(jnp.float32) >= radius).astype(jnp.float32)


def pencil_body(intensity, punch_radius):
    row_count = lax.axis_size("row")
    col_count = lax.axis_size("col")
    row_at = lax.axis_index("row")
    col_at = lax.axis_index("col")
    planes, h_block, k_block = intensity.shape
    groups = col_count // row_count
    fine_width = k_block // col_count
    pencil_rows = groups * fine_width
    levels = jnp.arange(planes, dtype=jnp.int32)
    swapped_table = jnp.swapaxes(punch_radius, 1, 2)
    outgoing = jnp.transpose(
        intensity.reshape(planes, h_block, col_count, fine_width), (2, 3, 0, 1)
    )
    arrived = lax.all_to_all(
        lax.all_to_all(outgoing, "col", split_axis=0, concat_axis=0, tiled=True),
        "row",
        split_axis=0,
        concat_axis=3,
        tiled=True,
    )
    pencil_h = (
        h_block * row_at
        + k_block * jnp.arange(groups, dtype=jnp.int32)[:, None]
        + fine_width * col_at
        + jnp.arange(fine_width, dtype=jnp.int32)[None, :]
    ).reshape(-1)
    whole_k = jnp.arange(N, dtype=jnp.int32)
    mirrored = arrived.reshape(pencil_rows, planes, N)
    pencil_input = jnp.transpose(
        intensity.reshape(planes, groups, col_count, fine_width, k_block), (1, 2, 3, 0, 4)
    )
    direct = lax.all_to_all(pencil_input, "col", split_axis=1, concat_axis=4, tiled=True).reshape(
        pencil_rows, planes, N
    )
    keep_mask = keep_map(pencil_h, whole_k, punch_radius, levels)
    keep_swap = keep_map(pencil_h, whole_k, swapped_table, levels)
    counts = jnp.maximum(keep_mask + keep_swap, 1.0)
    symmetric = ((keep_mask * direct + keep_swap * mirrored) / counts).astype(jnp.bfloat16)
    row_total = pencil_rows * planes
    flat_rows = symmetric.reshape(row_total, N).astype(jnp.float32)
    part_re, part_im = spectral_lead(flat_rows)
    freq_width = N // (row_count * col_count)
    sectioned = jnp.stack([part_re, part_im]).reshape(
        2, row_count, col_count, freq_width, row_total
    )
    spectra = lax.all_to_all(
        lax.all_to_all(sectioned, "row", split_axis=1, concat_axis=1, tiled=True),
        "col",
        split_axis=2,
        concat_axis=2,
        tiled=True,
    )
    spectra = spectra.reshape(2, row_count, col_count, freq_width, groups, fine_width, planes)
    spectra = jnp.transpose(spectra, (0, 6, 3, 1, 4, 2, 5)).reshape(2, planes * freq_width, N)
    final_re, final_im = spectral(spectra[0], spectra[1])
    out_re = (final_re / N).reshape(planes, freq_width, N)
    out_im = (final_im / N).reshape(planes, freq_width, N)
    return (out_re, out_im)


RADIX = 4
SHARES = 2


def spin(first_ids, second_ids, period):
    phases = first_ids * second_ids % period
    angles = phases.astype(jnp.float32) * (2.0 * math.pi / period)
    return jnp.cos(angles), jnp.sin(angles)


def halves(values):
    high = lax.reduce_precision(values, exponent_bits=8, mantissa_bits=7)
    return high.astype(jnp.bfloat16), (values - high).astype(jnp.bfloat16)


def packed(coarse, fine, shape):
    coarse_re, coarse_im = coarse
    fine_re, fine_im = fine
    full_re = (coarse_re * fine_re - coarse_im * fine_im).reshape(shape)
    full_im = (coarse_re * fine_im + coarse_im * fine_re).reshape(shape)
    return jnp.stack([*halves(full_re), *halves(full_im)])


def twiddles(length, owners, shares):
    width = length // RADIX
    fine = 16
    ids = jnp.arange(width, dtype=jnp.int32)
    lead = jnp.arange(RADIX, dtype=jnp.int32)[:, None, None, None]
    high_ids = (jnp.arange(width // fine, dtype=jnp.int32) * fine)[None, :, None, None]
    low_ids = jnp.arange(fine, dtype=jnp.int32)[None, None, :, None]
    minor = ids[None, None, None, :]
    shape = (RADIX, width, width)
    sample = RADIX * minor + lead
    block = high_ids.reshape(owners, shares, -1)
    turned = jnp.swapaxes(block, 0, 1).reshape(high_ids.shape)
    freq_major = packed(spin(sample, turned, length), spin(sample, low_ids, length), shape)
    time_major = packed(
        spin(RADIX * high_ids, minor, length), spin(RADIX * low_ids + lead, minor, length), shape
    )
    return freq_major, time_major


def dot32(left, right):
    return jnp.dot(left, right, preferred_element_type=jnp.float32)


def symmetrize(direct_ref, mirror_ref, near_ref, far_ref, pick_ref, order_ref, flip_ref, sym_ref):
    groups, _, block, width = direct_ref.shape
    rows = lax.broadcasted_iota(jnp.int32, (block, width), 0)
    cols = lax.broadcasted_iota(jnp.int32, (block, width), 1)
    row_off = (rows + SP // 2) % SP - SP // 2
    col_off = (cols + SP // 2) % SP - SP // 2
    distance = (row_off * row_off + col_off * col_off).astype(jnp.float32)
    merged = []
    for part in range(groups):
        picked = pick_ref[:, part * width : (part + 1) * width]
        keep_mirror = distance >= dot32(near_ref[0], picked)
        keep_direct = distance >= dot32(far_ref[0], picked)
        turned = jnp.concatenate(
            [
                direct_ref[piece, 0, part * width : (part + 1) * width, :].T
                for piece in range(groups)
            ],
            axis=0,
        )
        total = jnp.where(keep_mirror, mirror_ref[0, part, 0], 0.0) + jnp.where(
            keep_direct, turned, 0.0
        )
        scale = jnp.where(keep_mirror & keep_direct, 0.5, 1.0)
        merged.append((total * scale).astype(jnp.bfloat16))
    sym = jnp.concatenate(merged, axis=1)
    sorted_rows = dot32(order_ref[...], sym).astype(jnp.bfloat16)
    sorted_both = dot32(sorted_rows, flip_ref[...]).astype(jnp.bfloat16)
    sym_ref[0] = sorted_both.reshape(sym_ref.shape[1:])


def butterfly(res, ims):
    even_re, odd_re = res[0] + res[2], res[0] - res[2]
    even_im, odd_im = ims[0] + ims[2], ims[0] - ims[2]
    pair_re, gap_re = res[1] + res[3], res[1] - res[3]
    pair_im, gap_im = ims[1] + ims[3], ims[1] - ims[3]
    out_re = (even_re + pair_re, odd_re - gap_im, even_re - pair_re, odd_re + gap_im)
    out_im = (even_im + pair_im, odd_im + gap_re, even_im - pair_im, odd_im - gap_re)
    return out_re, out_im


def transform_first(table_ref, sym_ref, part_ref):
    res, ims = [], []
    for lead in range(RADIX):
        data = sym_ref[0, lead]
        res.append(dot32(table_ref[0, lead], data) + dot32(table_ref[1, lead], data))
        ims.append(dot32(table_ref[2, lead], data) + dot32(table_ref[3, lead], data))
    out_re, out_im = butterfly(res, ims)
    for block in range(RADIX):
        part_ref[block, 0, 0] = out_re[block].astype(part_ref.dtype)
        part_ref[block, 1, 0] = out_im[block].astype(part_ref.dtype)


def transform_second(scale, part_ref, table_ref, out_ref):
    sources, _, _, _, width = part_ref.shape
    piece = width // RADIX
    res, ims = [], []
    for lead in range(RADIX):
        data_re, data_im = (
            jnp.concatenate(
                [
                    part_ref[source, which, 0, :, lead * piece : (lead + 1) * piece]
                    for source in range(sources)
                ],
                axis=1,
            )
            for which in range(2)
        )
        res.append(
            dot32(data_re, table_ref[0, lead])
            + dot32(data_re, table_ref[1, lead])
            - dot32(data_im, table_ref[2, lead])
            - dot32(data_im, table_ref[3, lead])
        )
        ims.append(
            dot32(data_re, table_ref[2, lead])
            + dot32(data_re, table_ref[3, lead])
            + dot32(data_im, table_ref[0, lead])
            + dot32(data_im, table_ref[1, lead])
        )
    out_re, out_im = butterfly(res, ims)
    owners, _, _, rows, _ = out_ref.shape
    for which, values in ((0, out_re), (1, out_im)):
        for block in range(RADIX):
            ready = (values[block] * scale).astype(out_ref.dtype)
            span = ready.shape[1]
            for owner in range(owners):
                out_ref[owner, which, 0, :, block * span : (block + 1) * span] = ready[
                    owner * rows : (owner + 1) * rows
                ]


def swap_kernel(send_ref, got_ref, stage, send_sem, recv_sem, local_sem):
    count = send_ref.shape[0]
    me = lax.axis_index("row")
    barrier = pltpu.get_barrier_semaphore()
    for step in range(1, count):
        pl.semaphore_signal(barrier, inc=1, device_id={"row": lax.rem(me + step, count)})
    pl.semaphore_wait(barrier, count - 1)
    copies = []
    for step in range(1, count):
        peer = lax.rem(me + step, count)
        copy = pltpu.make_async_remote_copy(
            src_ref=send_ref.at[peer],
            dst_ref=got_ref.at[me],
            send_sem=send_sem.at[step - 1],
            recv_sem=recv_sem.at[step - 1],
            device_id={"row": peer},
        )
        copy.start()
        copies.append(copy)
    load = pltpu.make_async_copy(send_ref.at[me], stage, local_sem.at[0])
    load.start()
    load.wait()
    store = pltpu.make_async_copy(stage, got_ref.at[me], local_sem.at[1])
    store.start()
    store.wait()
    for copy in copies:
        copy.wait()


def swap(values, identity):
    count = values.shape[0]
    return pl.pallas_call(
        swap_kernel,
        out_shape=jax.ShapeDtypeStruct(values.shape, values.dtype),
        in_specs=[pl.BlockSpec(memory_space=pl.ANY)],
        out_specs=pl.BlockSpec(memory_space=pl.ANY),
        scratch_shapes=[
            pltpu.VMEM(values.shape[1:], values.dtype),
            pltpu.SemaphoreType.DMA((count - 1,)),
            pltpu.SemaphoreType.DMA((count - 1,)),
            pltpu.SemaphoreType.DMA((2,)),
        ],
        compiler_params=pltpu.CompilerParams(collective_id=identity, has_side_effects=True),
        cost_estimate=pl.CostEstimate(
            flops=40 * 10**9, bytes_accessed=values.size * 4, transcendentals=0
        ),
    )(values)


def widen_kernel(got_ref, *refs):
    re_ref, im_ref = refs[-2:]
    re_ref[0, 0] = got_ref[0, 0, 0].astype(jnp.float32)
    im_ref[0, 0] = got_ref[0, 1, 0].astype(jnp.float32)


def widen(at, share, held, received, outs):
    owners, _, _, rows, length = received.shape
    shape = jax.ShapeDtypeStruct((owners, held, rows * SHARES, length), jnp.float32)
    spec = pl.BlockSpec((1, 1, rows, length), lambda c: (c, at, share, 0))
    return pl.pallas_call(
        widen_kernel,
        out_shape=(shape, shape),
        grid=(owners,),
        in_specs=[pl.BlockSpec((1, 2, 1, rows, length), lambda c: (c, 0, 0, 0, 0))]
        + [pl.BlockSpec(memory_space=pl.ANY)] * len(outs),
        out_specs=(spec, spec),
        input_output_aliases={1 + which: which for which in range(len(outs))},
        cost_estimate=pl.CostEstimate(
            flops=8 * 10**9, bytes_accessed=received.size * 6, transcendentals=0
        ),
    )(received, *outs)


LIMIT = 56 * 1024 * 1024


def plane_body(intensity, punch_radius):
    row_count = lax.axis_size("row")
    col_count = lax.axis_size("col")
    row_at = lax.axis_index("row")
    col_at = lax.axis_index("col")
    planes, h_block, k_block = intensity.shape
    held = planes // col_count
    groups = h_block // k_block
    length = h_block * row_count
    width = length // RADIX
    piece = h_block // RADIX
    freq_width = length // (row_count * col_count)
    bf16 = jnp.bfloat16

    levels = held * col_at + jnp.arange(held, dtype=jnp.int32)
    plane_node = (levels + SP // 2) // SP
    plane_off = levels - SP * plane_node
    level_ids = jnp.arange(punch_radius.shape[0], dtype=jnp.int32)
    chosen = (plane_node[:, None] == level_ids[None, :]).astype(jnp.int32)
    table = jnp.sum(chosen[:, :, None, None] * punch_radius[None], axis=1)
    table = (table - (plane_off * plane_off)[:, None, None]).astype(bf16)
    node_count = punch_radius.shape[1]
    node_ids = jnp.arange(node_count, dtype=jnp.int32)
    whole = jnp.arange(length, dtype=jnp.int32)
    pick_k = ((whole[:, None] + SP // 2) // SP == node_ids[None, :]).astype(bf16)
    mine = h_block * row_at + jnp.arange(h_block, dtype=jnp.int32)
    pick_h = ((mine[None, :] + SP // 2) // SP == node_ids[:, None]).astype(bf16)
    near = jnp.einsum("kn,lnm->lkm", pick_k, table, preferred_element_type=jnp.float32)
    far = jnp.einsum("kn,lmn->lkm", pick_k, table, preferred_element_type=jnp.float32)
    near, far = near.astype(bf16), far.astype(bf16)
    local = jnp.arange(h_block, dtype=jnp.int32)
    source = RADIX * (local % piece) + local // piece
    order = (source[:, None] == local[None, :]).astype(bf16)
    flip = (source[None, :] == local[:, None]).astype(bf16)
    freq_major, time_major = twiddles(length, col_count, SHARES)

    span = freq_width // SHARES
    part_rows = width // SHARES
    tile = min(128, part_rows)
    owners = tile // span
    params = pltpu.CompilerParams(vmem_limit_bytes=LIMIT)
    split = intensity.reshape(col_count, held, h_block, k_block)

    def gather(at):
        return lax.all_to_all(split[:, at], "col", split_axis=0, concat_axis=0, tiled=True)

    def blend(at, direct, mirror):
        return pl.pallas_call(
            symmetrize,
            out_shape=jax.ShapeDtypeStruct((1, RADIX, width, h_block), bf16),
            grid=(1, row_count),
            in_specs=[
                pl.BlockSpec((groups, 1, h_block, k_block), lambda p, r: (r, p, 0, 0)),
                pl.BlockSpec((1, groups, 1, h_block, k_block), lambda p, r: (r, 0, p, 0, 0)),
                pl.BlockSpec((1, h_block, node_count), lambda p, r: (p, r, 0)),
                pl.BlockSpec((1, h_block, node_count), lambda p, r: (p, r, 0)),
                pl.BlockSpec((node_count, h_block), lambda p, r: (0, 0)),
                pl.BlockSpec((h_block, h_block), lambda p, r: (0, 0)),
                pl.BlockSpec((h_block, h_block), lambda p, r: (0, 0)),
            ],
            out_specs=pl.BlockSpec((1, RADIX, piece, h_block), lambda p, r: (p, 0, r, 0)),
            compiler_params=params,
            cost_estimate=pl.CostEstimate(
                flops=14 * 10**9, bytes_accessed=10**7, transcendentals=0
            ),
        )(
            direct.reshape(col_count, 1, h_block, k_block),
            mirror.reshape(row_count, groups, 1, h_block, k_block),
            near[at : at + 1],
            far[at : at + 1],
            pick_h,
            order,
            flip,
        )

    def first(share, sym):
        skip = share * (part_rows // tile)
        return pl.pallas_call(
            transform_first,
            out_shape=jax.ShapeDtypeStruct((RADIX, 2, 1, part_rows, h_block), bf16),
            grid=(part_rows // tile, 1),
            in_specs=[
                pl.BlockSpec((4, RADIX, tile, width), lambda d, p: (0, 0, d + skip, 0)),
                pl.BlockSpec((1, RADIX, width, h_block), lambda d, p: (p, 0, 0, 0)),
            ],
            out_specs=pl.BlockSpec((RADIX, 2, 1, tile, h_block), lambda d, p: (0, 0, p, d, 0)),
            compiler_params=params,
            cost_estimate=pl.CostEstimate(
                flops=14 * 10**9, bytes_accessed=10**7, transcendentals=0
            ),
        )(freq_major, sym)

    def second(parts):
        return pl.pallas_call(
            lambda *refs: transform_second(1.0 / length, *refs),
            out_shape=jax.ShapeDtypeStruct((col_count, 2, 1, span, length), bf16),
            grid=(1, part_rows // tile),
            in_specs=[
                pl.BlockSpec((row_count, 2, 1, tile, h_block), lambda p, d: (0, 0, p, d, 0)),
                pl.BlockSpec((4, RADIX, width, width), lambda p, d: (0, 0, 0, 0)),
            ],
            out_specs=pl.BlockSpec(
                (owners, 2, 1, span, length), lambda p, d: (d, 0, p, 0, 0)
            ),
            compiler_params=params,
            cost_estimate=pl.CostEstimate(
                flops=14 * 10**9, bytes_accessed=10**7, transcendentals=0
            ),
        )(parts, time_major)

    def deliver(sent):
        return lax.all_to_all(sent, "col", split_axis=0, concat_axis=0, tiled=True)

    directs = [gather(at) for at in range(held)]
    outs, waiting = (), None
    for at in range(held):
        direct = directs[at]
        mirror = swap(direct.reshape(row_count, groups, h_block, k_block), 0)
        if waiting is not None:
            mirror, received = lax.optimization_barrier((mirror, waiting[2]))
            outs = widen(waiting[0], waiting[1], held, received, outs)
        sym = blend(at, direct, mirror)
        waiting = None
        for share in range(SHARES):
            sent = second(swap(first(share, sym), 1))
            if at + 1 < held:
                sym, sent, directs[at + 1] = lax.optimization_barrier(
                    (sym, sent, directs[at + 1])
                )
            else:
                sym, sent = lax.optimization_barrier((sym, sent))
            received = deliver(sent)
            if share == 0 and at + 1 < held:
                waiting = (at, share, received)
            else:
                outs = widen(at, share, held, received, outs)
    return tuple(half.reshape(planes, freq_width, length) for half in outs)


def body(intensity, punch_radius):
    by_plane = lax.axis_size("row") == RADIX and intensity.shape[0] % lax.axis_size("col") == 0
    return (plane_body if by_plane else pencil_body)(intensity, punch_radius)


def solution(mesh):
    in_specs = (P(None, "row", "col"), P())
    out_specs = (P(None, ("row", "col"), None), P(None, ("row", "col"), None))
    return jax.shard_map(body, mesh=mesh, in_specs=in_specs, out_specs=out_specs, check_vma=False)
```
